256 devices in a mesh: seq: 128 (over z_lo, x, y, core), head: 2 (over z_hi).
Axes of the slice: x: 4, y: 4, z: 8 (z_hi: 2, z_lo: 4; z = z_hi * 4 + z_lo), core: 2. Of those that a mesh axis runs over, the one named last changes fastest.
Arguments:
- query_proj: bfloat16 [16384, 4096], P('seq', 'head'), as said below
- key_proj: bfloat16 [16384, 4096], P('seq', 'head'), as said below
- value_proj: bfloat16 [16384, 4096], P('seq', 'head'), may hold values from -6 to 6
- norm_grad: bfloat16 [16384, 4096], P('seq', 'head'), may hold values from -6 to 6
- norm_gain: float32 [4096], P('head'), may hold values from 0.25 to 1.75
- head_offsets: int32 [5, 32], P(None, 'head'), may hold values from 0 to 15, as said below
Outputs:
- query_grad: bfloat16 [16384, 4096], P('seq', 'head')
- key_grad: bfloat16 [16384, 4096], P('seq', 'head')
- value_grad: bfloat16 [16384, 4096], P('seq', 'head')
The draws below stay inside these ranges and needn't reach their ends.
Inputs may be any that keep to these rules, and one draw needn't show every extreme that they name: `query_proj`: entries lie between -8 and 8. `key_proj`: entries lie between -8 and 8. head_offsets[l, h] is below 2^l; at every level l each value below min(32, 2^l) belongs to some head.
All inputs are finite; a program needn't handle non-finite values.
Results may differ from the reference program's by a relative error of at most 0.0069.
The reference program's roundings to bfloat16 on the way count: a program that leaves them out, or rounds other values in their place, can miss the bound.
Values may be sent and summed in bfloat16 or wider, within the bound.
No kernel may reach another device: no remote copies, remote signals or barrier semaphores. Data moves between devices by JAX's collectives and lax.ppermute only.
A program may use at most 128 MiB of HBM per device.

```python
import jax
import jax.numpy as jnp
from jax import lax

WIDTH = 4096
HEADS = 32
HEAD_DIM = 128
LEVELS = 5
TOK_DEV = 128
TOKENS = 16384


def drawn_draw(key, which):
    full_width = HEADS * HEAD_DIM
    drawn = jax.random.normal(jax.random.fold_in(key, which), (TOKENS, full_width), jnp.float32)
    drawn = jnp.clip(drawn, -4.0, 4.0)
    return drawn


def draw_query_proj(key, part):
    return drawn_draw(key, 11).astype(jnp.bfloat16)


def draw_key_proj(key, part):
    return drawn_draw(key, 23).astype(jnp.bfloat16)


def draw_head_offsets(key, part):
    table = []
    for degree in range(LEVELS):
        order = jax.random.permutation(jax.random.fold_in(key, 300 + degree), HEADS)
        table.append(order % 2 ** degree)
    return jnp.stack(table).astype(jnp.int32)


def shard_levels(own_key, shape, shards, smallest, high):
    loudness, own = 1.0, jax.random.fold_in(own_key, 6)
    for position, parts in shards:
        steps = jnp.exp(jax.random.uniform(jax.random.fold_in(own, position), (parts,), jnp.float32, smallest / len(shards), high / len(shards)))
        loudness = loudness * jnp.repeat(steps, shape[position] // parts).reshape([-1 if axis == position else 1 for axis in range(len(shape))])
    return loudness


def scatter_about(key, extent, scale, most, cuts=(), held_as=jnp.bfloat16):
    entries = scale * jax.random.normal(key, extent, jnp.float32)
    if cuts:
        entries = entries * shard_levels(key, extent, cuts, -0.22, 0.18)
    return jnp.clip(entries, -most, most).astype(held_as)


def setup_inputs(seed: int = 0) -> dict:
    key_of = jax.random.split(jax.random.key(seed), 7)
    query_proj = draw_query_proj(jax.random.fold_in(key_of[6], 71), 0)
    key_proj = draw_key_proj(jax.random.fold_in(key_of[6], 71), 0)
    value_proj = scatter_about(key_of[2], (TOKENS, WIDTH), 1.0, 6.0, ((0, 128), (1, 2)))
    norm_grad = scatter_about(key_of[3], (TOKENS, WIDTH), 1.0, 6.0, ((0, 128), (1, 2)))
    norm_gain = jnp.clip(1.0 + 0.15 * jax.random.normal(key_of[4], (WIDTH,), jnp.float32), 0.25, 1.75)
    head_offsets = draw_head_offsets(jax.random.fold_in(key_of[6], 71), 0)
    return dict(query_proj=query_proj, key_proj=key_proj, value_proj=value_proj, norm_grad=norm_grad, norm_gain=norm_gain, head_offsets=head_offsets)


EPSILON = 1e-05
FAR_BELOW = -1e+30

def rounded(number):
    return lax.optimization_barrier(number.astype(jnp.bfloat16)).astype(jnp.float32)

def chooser(offsets_row, stride):
    return jnp.arange(stride, dtype=jnp.int32)[:, None] == offsets_row.astype(jnp.int32)[None, :]

def pick_rows(source, chosen):
    stride = chosen.shape[0]
    shaped = source.reshape(source.shape[0] // stride, stride, HEADS, HEAD_DIM)
    picked = lax.optimization_barrier(jnp.sum(shaped * chosen.astype(source.dtype)[None, :, :, None], axis=1))
    return picked.astype(source.dtype)

def pick_stats(source, chosen):
    stride = chosen.shape[0]
    shaped = source.reshape(source.shape[0] // stride, stride, HEADS)
    return lax.optimization_barrier(jnp.sum(shaped * chosen.astype(source.dtype)[None], axis=1))

def put_rows(values, chosen):
    stride = chosen.shape[0]
    spread = values[:, None] * chosen.astype(values.dtype)[None, :, :, None]
    return spread.reshape(values.shape[0] * stride, HEADS * HEAD_DIM)

def put_stats(values, chosen, fill_value):
    stride = chosen.shape[0]
    spread = jnp.where(chosen[None], values[:, None, :], fill_value)
    return spread.reshape(values.shape[0] * stride, HEADS)

def segmented(source):
    return source.reshape(source.shape[0] // TOK_DEV, TOK_DEV, *source.shape[1:])

def segment_scores(query_blk, key_blk):
    scored = jnp.einsum('qhd,khd->hqk', query_blk.astype(jnp.float32), key_blk.astype(jnp.float32))
    return scored * HEAD_DIM ** (-0.5)

def moments_block(items):
    scored = segment_scores(items[0], items[1])
    row_peak = lax.optimization_barrier(jnp.max(scored, axis=2))
    row_total = lax.optimization_barrier(jnp.sum(jnp.exp(scored - row_peak[:, :, None]), axis=2))
    return (row_peak.T, row_total.T)

def output_block(items):
    query_blk, key_blk, value_blk, norm_blk = items
    probs = jnp.exp(segment_scores(query_blk, key_blk) - norm_blk.T[:, :, None])
    return jnp.einsum('hqk,khd->qhd', rounded(probs), value_blk.astype(jnp.float32))

def delta_block(items):
    query_blk, key_blk, value_blk, norm_blk, grad_blk = items
    probs = jnp.exp(segment_scores(query_blk, key_blk) - norm_blk.T[:, :, None])
    slope_block = jnp.einsum('qhd,khd->hqk', grad_blk.astype(jnp.float32), value_blk.astype(jnp.float32))
    return lax.optimization_barrier(jnp.sum(probs * slope_block, axis=2)).T

def gradient_block(items):
    query_blk, key_blk, value_blk, norm_blk, grad_blk, delta_blk = items
    probs = jnp.exp(segment_scores(query_blk, key_blk) - norm_blk.T[:, :, None])
    slope_block = jnp.einsum('qhd,khd->hqk', grad_blk.astype(jnp.float32), value_blk.astype(jnp.float32))
    pushed = rounded(probs * (slope_block - delta_blk.T[:, :, None]) * HEAD_DIM ** (-0.5))
    query_part = jnp.einsum('hqk,khd->qhd', pushed, key_blk.astype(jnp.float32))
    key_part = jnp.einsum('hqk,qhd->khd', pushed, query_blk.astype(jnp.float32))
    value_part = jnp.einsum('hqk,qhd->khd', rounded(probs), grad_blk.astype(jnp.float32))
    return (query_part, key_part, value_part)

def reference(query_proj, key_proj, value_proj, norm_grad, norm_gain, head_offsets):
    choosers = [chooser(head_offsets[degree], 2 ** degree) for degree in range(LEVELS)]
    query_seg = [segmented(pick_rows(query_proj, chosen)) for chosen in choosers]
    key_seg = [segmented(pick_rows(key_proj, chosen)) for chosen in choosers]
    value_seg = [segmented(pick_rows(value_proj, chosen)) for chosen in choosers]
    peak_rows = []
    total_rows = []
    for degree in range(LEVELS):
        peak_seg, total_seg = lax.map(moments_block, (query_seg[degree], key_seg[degree]))
        peak_rows.append(put_stats(peak_seg.reshape(-1, HEADS), choosers[degree], FAR_BELOW))
        total_rows.append(put_stats(total_seg.reshape(-1, HEADS), choosers[degree], 0.0))
    highest = peak_rows[0]
    for degree in range(1, LEVELS):
        highest = jnp.maximum(highest, peak_rows[degree])
    summed = total_rows[0] * jnp.exp(peak_rows[0] - highest)
    for degree in range(1, LEVELS):
        summed = summed + total_rows[degree] * jnp.exp(peak_rows[degree] - highest)
    log_norm = highest + jnp.log(summed)
    norm_seg = [segmented(pick_stats(log_norm, chosen)) for chosen in choosers]
    attention = jnp.zeros((TOKENS, WIDTH), jnp.float32)
    for degree in range(LEVELS):
        partial_value = lax.map(output_block, (query_seg[degree], key_seg[degree], value_seg[degree], norm_seg[degree]))
        attention = attention + put_rows(partial_value.reshape(-1, HEADS, HEAD_DIM), choosers[degree])
    center = lax.optimization_barrier(jnp.mean(attention, axis=1))
    spread_var = lax.optimization_barrier(jnp.mean(attention * attention, axis=1)) - center * center
    inverse = lax.rsqrt(spread_var + EPSILON)
    normed = (attention - center[:, None]) * inverse[:, None]
    scaled = norm_grad.astype(jnp.float32) * norm_gain[None, :]
    first_mean = lax.optimization_barrier(jnp.mean(scaled, axis=1))
    second_mean = lax.optimization_barrier(jnp.mean(scaled * normed, axis=1))
    attn_grad = (inverse[:, None] * (scaled - first_mean[:, None] - normed * second_mean[:, None])).astype(jnp.bfloat16)
    grad_seg = [segmented(pick_rows(attn_grad, chosen)) for chosen in choosers]
    delta = jnp.zeros((TOKENS, HEADS), jnp.float32)
    for degree in range(LEVELS):
        partial_value = lax.map(delta_block, (query_seg[degree], key_seg[degree], value_seg[degree], norm_seg[degree], grad_seg[degree]))
        delta = delta + put_stats(partial_value.reshape(-1, HEADS), choosers[degree], 0.0)
    delta_seg = [segmented(pick_stats(delta, chosen)) for chosen in choosers]
    query_acc = jnp.zeros((TOKENS, WIDTH), jnp.float32)
    key_acc = jnp.zeros((TOKENS, WIDTH), jnp.float32)
    value_acc = jnp.zeros((TOKENS, WIDTH), jnp.float32)
    for degree in range(LEVELS):
        query_part, key_part, value_part = lax.map(gradient_block, (query_seg[degree], key_seg[degree], value_seg[degree], norm_seg[degree], grad_seg[degree], delta_seg[degree]))
        query_acc = query_acc + put_rows(query_part.reshape(-1, HEADS, HEAD_DIM), choosers[degree])
        key_acc = key_acc + put_rows(key_part.reshape(-1, HEADS, HEAD_DIM), choosers[degree])
        value_acc = value_acc + put_rows(value_part.reshape(-1, HEADS, HEAD_DIM), choosers[degree])
    return (query_acc.astype(jnp.bfloat16), key_acc.astype(jnp.bfloat16), value_acc.astype(jnp.bfloat16))
```

```python
import jax
import jax.numpy as jnp
from jax import lax
from jax.experimental import pallas as pl
from jax.experimental.pallas import tpu as pltpu
from jax.sharding import PartitionSpec as P

WIDTH = 4096
HEAD_DIM = 128
LEVELS = 5
TOK = 128
EPSILON = 1e-05
FAR_BELOW = -1e30
SCALE = HEAD_DIM ** (-0.5)
PAIR = 2

FAR_MASKS = {1: (), 2: (2,), 3: (2, 6), 4: (2, 6, 8)}


F32 = jnp.float32
BF16 = jnp.bfloat16


def rows_of(level):
    return TOK // 2**level


def far_parts(level):
    return 2 ** (level - 1)


def swapped(value, mask):
    pairs = [(source, source ^ mask) for source in range(lax.axis_size("seq"))]
    return lax.ppermute(value, "seq", pairs)


def dot(left, right, left_dim, right_dim):
    return lax.dot_general(
        left, right, (((left_dim,), (right_dim,)), ((), ())), preferred_element_type=F32
    )


def target_of(index, offsets):
    found = jnp.full_like(index, -1)
    start = 0
    for level in range(1, LEVELS):
        count = rows_of(level)
        inside = (index >= start) & (index < start + count)
        found = jnp.where(inside, (index - start) * 2**level + offsets[level], found)
        start += count
    return found


def offsets_at(off_ref, head):
    return [off_ref[level, head] for level in range(LEVELS)]


def head_cols(ref, inner):
    return ref[:, inner * HEAD_DIM : (inner + 1) * HEAD_DIM]


def pick_kernel(off_ref, key_ref, value_ref, *out_refs):
    step = pl.program_id(0)
    index = lax.broadcasted_iota(jnp.int32, (TOK, TOK), 0)
    token = lax.broadcasted_iota(jnp.int32, (TOK, TOK), 1)
    for inner in range(PAIR):
        offsets = offsets_at(off_ref, step * PAIR + inner)
        chosen = jnp.where(target_of(index, offsets) == token, 1.0, 0.0).astype(BF16)
        both = jnp.concatenate([head_cols(key_ref, inner), head_cols(value_ref, inner)], axis=1)
        picked = dot(chosen, both, 1, 0)
        start = 0
        for level in range(1, LEVELS):
            count = rows_of(level)
            piece = picked[start : start + count]
            out_refs[level - 1][0, inner] = jnp.concatenate(
                [piece[:, :HEAD_DIM], piece[:, HEAD_DIM:]], axis=0
            ).astype(BF16)
            start += count


def split_rows(block, level):
    count = rows_of(level)
    if level == LEVELS - 1:
        block = block.astype(F32)
    return block[:count], block[count:]


def segment_rows(near_ref, far_ref, inner, level):
    keys, values = [], []
    for ref in (near_ref, far_ref):
        for part in range(far_parts(level)):
            key, value = split_rows(ref[part, inner], level)
            keys.append(key)
            values.append(value)
    return (
        jnp.concatenate(keys, axis=0).astype(BF16),
        jnp.concatenate(values, axis=0).astype(BF16),
    )


def all_rows(key_ref, value_ref, part_refs, inner):
    rows = [(head_cols(key_ref, inner), head_cols(value_ref, inner))]
    for level in range(1, LEVELS):
        rows.append(
            segment_rows(part_refs[2 * level - 2], part_refs[2 * level - 1], inner, level)
        )
    return rows


def masked_scores(keys, query, offsets):
    token = lax.broadcasted_iota(jnp.int32, (1, TOK), 1)
    scores = []
    for level in range(LEVELS):
        scored = dot(keys[level], query, 1, 1) * SCALE
        if level:
            chosen = (token & (2**level - 1)) == offsets[level]
            scored = scored + jnp.where(chosen, 0.0, FAR_BELOW)
        scores.append(scored)
    return scores


def added(pieces):
    total = pieces[0]
    for piece in pieces[1:]:
        total = total + piece
    return total


def forward_kernel(off_ref, query_ref, key_ref, value_ref, grad_ref, gain_ref, *refs):
    part_refs = refs[:8]
    attn_ref, norm_ref, stat_ref, sums_ref = refs[8:]
    step = pl.program_id(0)

    @pl.when(step == 0)
    def _():
        sums_ref[...] = jnp.zeros_like(sums_ref)

    for inner in range(PAIR):
        offsets = offsets_at(off_ref, step * PAIR + inner)
        rows = all_rows(key_ref, value_ref, part_refs, inner)
        scores = masked_scores([row[0] for row in rows], head_cols(query_ref, inner), offsets)
        highest = scores[0]
        for scored in scores[1:]:
            highest = jnp.maximum(highest, scored)
        peak = jnp.max(highest, axis=0, keepdims=True)
        raised = [jnp.exp(scored - peak) for scored in scores]
        total = jnp.sum(added(raised), axis=0, keepdims=True)
        norm_ref[0, inner : inner + 1] = peak + jnp.log(total)
        inverse = 1.0 / total
        attention = added(
            [
                dot((raised[level] * inverse).astype(BF16), rows[level][1], 0, 0)
                for level in range(LEVELS)
            ]
        )
        attn_ref[:, inner * HEAD_DIM : (inner + 1) * HEAD_DIM] = attention
        scaled = head_cols(grad_ref, inner).astype(F32) * head_cols(gain_ref, inner)
        sums_ref[0] += attention
        sums_ref[1] += attention * attention
        sums_ref[2] += scaled
        sums_ref[3] += scaled * attention

    @pl.when(step == pl.num_programs(0) - 1)
    def _():
        lane = lax.broadcasted_iota(jnp.int32, (TOK, TOK), 1)
        table = jnp.zeros((TOK, TOK), F32)
        for which in range(4):
            table = jnp.where(lane == which, jnp.sum(sums_ref[which], axis=1, keepdims=True), table)
        stat_ref[...] = table.T[:8]


def backward_kernel(off_ref, query_ref, key_ref, value_ref, grad_ref, gain_ref, *refs):
    part_refs = refs[:8]
    attn_ref, norm_ref, own_ref, other_ref = refs[8:12]
    query_out, key_out, value_out = refs[12:15]
    out_refs = refs[15:23]
    cols_ref = refs[23]
    step = pl.program_id(0)

    @pl.when(step == 0)
    def _():
        means = (own_ref[...] + other_ref[...]) * (1.0 / WIDTH)
        center = means[0:1]
        inverse = lax.rsqrt(means[1:2] - center * center + EPSILON)
        first = means[2:3]
        second = inverse * (means[3:4] - center * first)
        sublane = lax.broadcasted_iota(jnp.int32, (TOK, TOK), 0)
        table = jnp.zeros((TOK, TOK), F32)
        for which, row in enumerate((center, inverse, first, second)):
            table = jnp.where(sublane == which, row, table)
        cols_ref[...] = table.T

    center = cols_ref[:, 0:1]
    inverse = cols_ref[:, 1:2]
    first = cols_ref[:, 2:3]
    second = cols_ref[:, 3:4]
    for inner in range(PAIR):
        cols = slice(inner * HEAD_DIM, (inner + 1) * HEAD_DIM)
        offsets = offsets_at(off_ref, step * PAIR + inner)
        rows = all_rows(key_ref, value_ref, part_refs, inner)
        query = head_cols(query_ref, inner)
        scaled = head_cols(grad_ref, inner).astype(F32) * head_cols(gain_ref, inner)
        normed = (head_cols(attn_ref, inner) - center) * inverse
        attn_grad = (inverse * (scaled - first - normed * second)).astype(BF16)
        scores = masked_scores([row[0] for row in rows], query, offsets)
        log_norm = norm_ref[0, inner : inner + 1]
        probs = [jnp.exp(scored - log_norm) for scored in scores]
        slopes = [dot(row[1], attn_grad, 1, 1) for row in rows]
        delta = jnp.sum(
            added([probs[level] * slopes[level] for level in range(LEVELS)]), axis=0, keepdims=True
        )
        pushed = [
            (probs[level] * (slopes[level] - delta) * SCALE).astype(BF16)
            for level in range(LEVELS)
        ]
        query_out[:, cols] = added(
            [dot(pushed[level], rows[level][0], 0, 0) for level in range(LEVELS)]
        ).astype(BF16)
        for level in range(LEVELS):
            key_part = dot(pushed[level], query, 1, 0)
            value_part = dot(probs[level].astype(BF16), attn_grad, 1, 0)
            if level == 0:
                key_out[:, cols] = key_part
                value_out[:, cols] = value_part
                continue
            count = rows_of(level)
            parts = far_parts(level)
            for place in range(2 * parts):
                piece = slice(place * count, (place + 1) * count)
                out_refs[2 * level - 2 + place // parts][place % parts, inner] = jnp.concatenate(
                    [key_part[piece], value_part[piece]], axis=0
                ).astype(BF16)


def finish_kernel(off_ref, key_ref, value_ref, *refs):
    part_refs = refs[:8]
    key_out, value_out = refs[8:]
    step = pl.program_id(0)
    index = lax.broadcasted_iota(jnp.int32, (TOK, TOK), 1)
    token = lax.broadcasted_iota(jnp.int32, (TOK, TOK), 0)
    for inner in range(PAIR):
        cols = slice(inner * HEAD_DIM, (inner + 1) * HEAD_DIM)
        offsets = offsets_at(off_ref, step * PAIR + inner)
        chosen = jnp.where(target_of(index, offsets) == token, 1.0, 0.0).astype(BF16)
        placed = []
        for side in range(2):
            keys, values = [], []
            for level in range(1, LEVELS):
                block = part_refs[2 * level - 2 + side][0, inner].astype(F32)
                count = rows_of(level)
                keys.append(block[:count])
                values.append(block[count:])
            unused = jnp.zeros((rows_of(LEVELS - 1), HEAD_DIM), F32)
            both = jnp.concatenate(
                [
                    jnp.concatenate(keys + [unused], axis=0),
                    jnp.concatenate(values + [unused], axis=0),
                ],
                axis=1,
            ).astype(BF16)
            placed.append(dot(chosen, both, 1, 0))
        total = placed[0] + placed[1]
        key_out[:, cols] = (key_ref[:, cols] + total[:, :HEAD_DIM]).astype(BF16)
        value_out[:, cols] = (value_ref[:, cols] + total[:, HEAD_DIM:]).astype(BF16)


def cols_spec():
    return pl.BlockSpec((TOK, PAIR * HEAD_DIM), lambda step: (0, step))


def part_spec(level, parts):
    return pl.BlockSpec((parts, PAIR, 2 * rows_of(level), HEAD_DIM), lambda step: (0, step, 0, 0))


def part_shape(level, parts, heads):
    return jax.ShapeDtypeStruct((parts, heads, 2 * rows_of(level), HEAD_DIM), BF16)


def whole_spec():
    return pl.BlockSpec((8, TOK), lambda step: (0, 0))


def shards(query_proj, key_proj, value_proj, norm_grad, norm_gain, head_offsets):
    heads = head_offsets.shape[1]
    steps = heads // PAIR
    wide = query_proj.shape[1]
    gain = norm_gain.reshape(1, wide)
    off_spec = pl.BlockSpec(memory_space=pltpu.SMEM)
    gain_spec = pl.BlockSpec((1, PAIR * HEAD_DIM), lambda step: (0, step))
    norm_spec = pl.BlockSpec((1, PAIR, TOK), lambda step: (step, 0, 0))
    levels = range(1, LEVELS)

    def call(kernel, in_specs, out_specs, out_shape, scratch, flops, size, name):
        return pl.pallas_call(
            kernel,
            grid=(steps,),
            in_specs=in_specs,
            out_specs=out_specs,
            out_shape=out_shape,
            scratch_shapes=scratch,
            compiler_params=pltpu.CompilerParams(dimension_semantics=("arbitrary",)),
            cost_estimate=pl.CostEstimate(flops=flops, bytes_accessed=size, transcendentals=0),
            name=name,
        )

    unit = heads * 2 * TOK**3
    own = call(
        pick_kernel,
        [off_spec, cols_spec(), cols_spec()],
        [part_spec(level, 1) for level in levels],
        [part_shape(level, 1, heads) for level in levels],
        [],
        2 * unit,
        2 << 20,
        "pick",
    )(head_offsets, key_proj, value_proj)

    held = dict(zip(levels, own))
    for place in range(3):
        for level in (4, 3, 2):
            if place < len(FAR_MASKS[level]):
                other = swapped(held[level], FAR_MASKS[level][place])
                held[level] = jnp.concatenate([held[level], other], axis=0)
    gathered = []
    for level in levels:
        gathered += [held[level], swapped(held[level], 1)]

    part_specs = []
    for level in levels:
        part_specs += [part_spec(level, far_parts(level))] * 2

    attention, log_norm, own_stats = call(
        forward_kernel,
        [off_spec] + [cols_spec()] * 4 + [gain_spec] + part_specs,
        [cols_spec(), norm_spec, whole_spec()],
        [
            jax.ShapeDtypeStruct((TOK, wide), F32),
            jax.ShapeDtypeStruct((steps, PAIR, TOK), F32),
            jax.ShapeDtypeStruct((8, TOK), F32),
        ],
        [pltpu.VMEM((4, TOK, TOK), F32)],
        10 * unit,
        7 << 20,
        "attend",
    )(head_offsets, query_proj, key_proj, value_proj, norm_grad, gain, *gathered)
    other_stats = lax.ppermute(own_stats, "head", [(0, 1), (1, 0)])

    part_shapes = []
    for level in levels:
        part_shapes += [part_shape(level, far_parts(level), heads)] * 2
    results = call(
        backward_kernel,
        [off_spec]
        + [cols_spec()] * 4
        + [gain_spec]
        + part_specs
        + [cols_spec(), norm_spec, whole_spec(), whole_spec()],
        [cols_spec()] * 3 + part_specs,
        [
            jax.ShapeDtypeStruct((TOK, wide), BF16),
            jax.ShapeDtypeStruct((TOK, wide), F32),
            jax.ShapeDtypeStruct((TOK, wide), F32),
        ]
        + part_shapes,
        [pltpu.VMEM((TOK, TOK), F32)],
        25 * unit,
        14 << 20,
        "gradient",
    )(
        head_offsets,
        query_proj,
        key_proj,
        value_proj,
        norm_grad,
        gain,
        *gathered,
        attention,
        log_norm,
        own_stats,
        other_stats,
    )
    query_grad, key_own, value_own = results[:3]

    kept = {level: results[3 + 2 * level - 2] for level in levels}
    sent = {level: results[3 + 2 * level - 1] for level in levels}
    masks = {level: list(FAR_MASKS[level]) for level in levels}
    final = {}
    for level in (4, 3, 2, 1):
        other = swapped(sent[level], 1)
        if masks[level]:
            kept[level] = (kept[level].astype(F32) + other.astype(F32)).astype(BF16)
        else:
            final[level] = (kept[level], other)
    for _ in range(3):
        for level in (4, 3, 2):
            if not masks[level]:
                continue
            mask = masks[level].pop()
            half = kept[level].shape[0] // 2
            other = swapped(kept[level][half:], mask)
            mine = kept[level][:half]
            if masks[level]:
                kept[level] = (mine.astype(F32) + other.astype(F32)).astype(BF16)
            else:
                final[level] = (mine, other)
    finals = []
    final_specs = []
    for level in levels:
        finals += list(final[level])
        final_specs += [part_spec(level, 1)] * 2
    key_grad, value_grad = call(
        finish_kernel,
        [off_spec] + [cols_spec()] * 2 + final_specs,
        [cols_spec()] * 2,
        [jax.ShapeDtypeStruct((TOK, wide), BF16)] * 2,
        [],
        4 * unit,
        4 << 20,
        "finish",
    )(head_offsets, key_own, value_own, *finals)
    return query_grad, key_grad, value_grad


def solution(mesh):
    in_specs = (
        P("seq", "head"),
        P("seq", "head"),
        P("seq", "head"),
        P("seq", "head"),
        P("head"),
        P(None, "head"),
    )
    out_specs = (P("seq", "head"), P("seq", "head"), P("seq", "head"))
    return jax.shard_map(shards, mesh=mesh, in_specs=in_specs, out_specs=out_specs, check_vma=False)
```
